768 devices in a mesh: row: 96 (over z, y_hi, core), col: 8 (over x, y_lo).
Axes of the slice: x: 4, y: 8 (y_hi: 4, y_lo: 2; y = y_hi * 2 + y_lo), z: 12, core: 2. Of those that a mesh axis runs over, the one named last changes fastest.
Arguments:
- features: bfloat16 [98304, 128], P(('row', 'col')), may hold values from -6 to 6
- tiles: bfloat16 [96, 8, 128, 128, 128], P('row', 'col'), may hold values from -0.0625 to 0.0625
- tile_index: int32 [96, 8, 128], P('row', 'col'), may hold values from 0 to 767, as said below
- tile_count: int32 [96, 8], P('row', 'col'), may hold values from 16 to 128, as said below
- w_first: bfloat16 [128, 256], replicated, may hold values from -0.5 to 0.5
- b_first: float32 [256], replicated, may hold values from -3 to 3
- w_second: bfloat16 [256, 128], replicated, may hold values from -0.375 to 0.375
- b_second: float32 [128], replicated, may hold values from -3 to 3
Outputs:
- logits: float32 [98304, 128], P(('row', 'col'))
The draws below stay inside these ranges and needn't reach their ends.
Inputs may be any that keep to these rules, and one draw needn't show every extreme that they name: `tile_index`: within one device the live slots name distinct tiles. `tile_count`: some device has all 128 slots live; every count is 128 divided by 1, 2, 4 or 8.
All inputs are finite; a program needn't handle non-finite values.
Results may differ from the reference program's by a relative error of at most 0.01.
Values may be sent and summed in bfloat16 or wider, within the bound.
No kernel may reach another device: no remote copies, remote signals or barrier semaphores. Data moves between devices by JAX's collectives and lax.ppermute only.
A program may use at most 32 MiB of HBM per device.

```python
import jax
import jax.numpy as jnp
from jax import lax

F_IN = 128
HID = 256
OUT = 128
TILE = 128
NODE_DEV = 128
RT = 8
CT = 96
MAXT = 128
NODES = 98304
N_ROW = 96
N_COL = 8


def draw_tile_index(key, part):
    keys = jax.random.split(key, N_ROW * N_COL)
    picked = jax.vmap(lambda one_key: jax.random.permutation(one_key, RT * CT)[:MAXT])(keys)
    return picked.reshape(N_ROW, N_COL, MAXT).astype(jnp.int32)


def draw_tile_count(key, part):
    halvings = jax.random.randint(key, (N_ROW * N_COL,), 0, 4)
    counts = jnp.right_shift(jnp.full((N_ROW * N_COL,), MAXT, jnp.int32), halvings.astype(jnp.int32))
    busiest = jax.random.randint(jax.random.fold_in(key, 7), (), 0, N_ROW * N_COL)
    counts = counts.at[busiest].set(MAXT)
    return counts.reshape(N_ROW, N_COL).astype(jnp.int32)


def levels(key, dims, cuts, low, top_value):
    def one(position, parts):
        heights = jax.random.uniform(jax.random.fold_in(jax.random.fold_in(key, 6), position), (parts,), jnp.float32, low / len(cuts), top_value / len(cuts))
        return jnp.repeat(jnp.exp(heights), dims[position] // parts).reshape((-1,) + (1,) * (len(dims) - position - 1))

    loudness = one(*cuts[0])
    for cut in cuts[1:]:
        loudness = loudness * one(*cut)
    return loudness


def gaussian(own_key, shape, spread, limit, shards=(), held_as=jnp.bfloat16):
    result = jax.random.normal(own_key, shape, jnp.float32) * spread
    if len(shards) > 0:
        result = levels(own_key, shape, shards, -0.22, 0.18) * result
    return jnp.clip(result, min=-limit, max=limit).astype(held_as)


def setup_inputs(seed: int = 0) -> dict:
    key_of = jax.random.split(jax.random.key(seed), 9)
    features = gaussian(key_of[0], (NODES, F_IN), 1.0, 6.0, ((0, 768),))
    tiles = gaussian(key_of[1], (N_ROW, N_COL, MAXT, TILE, TILE), (TILE * MAXT * N_COL // (2 * RT)) ** -0.5, 0.0625, ((0, 96), (1, 8)))
    tile_index = draw_tile_index(jax.random.fold_in(key_of[8], 71), 0)
    tile_count = draw_tile_count(jax.random.fold_in(key_of[8], 71), 0)
    w_first = gaussian(key_of[4], (F_IN, HID), F_IN ** -0.5, 0.5)
    b_first = gaussian(key_of[5], (HID,), 0.5, 3.0, (), jnp.float32)
    w_second = gaussian(key_of[6], (HID, OUT), HID ** -0.5, 0.375)
    b_second = gaussian(key_of[7], (OUT,), 0.5, 3.0, (), jnp.float32)
    return {"features": features, "tiles": tiles, "tile_index": tile_index, "tile_count": tile_count, "w_first": w_first, "b_first": b_first, "w_second": w_second, "b_second": b_second}


def aggregate(tiles, tile_index, tile_count, node_feats):
    feat_width = node_feats.shape[1]
    col_blocks = node_feats.reshape(N_ROW, N_COL, NODE_DEV, feat_width).transpose(1, 0, 2, 3).reshape(N_COL, CT, TILE, feat_width)

    def one_device(packed):
        tile_block, slot_index, live_count, col_tiles = packed
        picked = jnp.take(col_tiles, slot_index % CT, axis=0).astype(jnp.float32)
        products = jnp.einsum("mab,mbf->maf", tile_block.astype(jnp.float32), picked)
        live_mask = jnp.arange(MAXT, dtype=jnp.int32) < live_count
        placing = (((slot_index // CT)[:, None] == jnp.arange(RT, dtype=jnp.int32)[None, :]) & live_mask[:, None]).astype(jnp.float32)
        return jnp.einsum("mr,maf->raf", placing, products).reshape(RT * TILE, feat_width)

    def one_row(packed):
        tile_row, index_row, count_row = packed
        partials = lax.map(one_device, (tile_row, index_row, count_row, col_blocks))
        return jnp.sum(partials, axis=0)

    row_sums = lax.map(one_row, (tiles, tile_index, tile_count))
    return row_sums.reshape(N_ROW * N_COL * NODE_DEV, feat_width)


def reference(features, tiles, tile_index, tile_count, w_first, b_first, w_second, b_second):
    agg_first = aggregate(tiles, tile_index, tile_count, features).astype(jnp.bfloat16)
    hidden = jnp.maximum(jnp.dot(agg_first, w_first, preferred_element_type=jnp.float32) + b_first, 0.0).astype(jnp.bfloat16)
    projected = jnp.dot(hidden, w_second, preferred_element_type=jnp.float32).astype(jnp.bfloat16)
    return aggregate(tiles, tile_index, tile_count, projected) + b_second
```

```python
import jax
import jax.numpy as jnp
from jax import lax
from jax.experimental import pallas as pl
from jax.experimental.pallas import tpu as pltpu
from jax.sharding import Mesh, PartitionSpec as P

TILE = 128
ROW_TILES = 8
SLOTS = 128
CHUNK = 16
UNROLL = 8
AXES = ("z", "yh", "core", "x", "yl")
SIZES = (12, 4, 2, 4, 2)
ROW = ("z", "yh", "core")
COL = ("x", "yl")


def spmm_kernel(count, rows, cols, tiles, *rest):
    pieces = rest[:4]
    out, tile_buf, feat, acc, sems = rest[4:]
    live = count[0]
    chunks = SLOTS // CHUNK

    def fetch(c):
        part = pl.ds(c * CHUNK, CHUNK)
        return pltpu.make_async_copy(tiles.at[part], tile_buf.at[part], sems.at[c])

    for c in range(chunks):
        @pl.when(c * CHUNK < live)
        def _():
            fetch(c).start()

    depth = pieces[0].shape[0]
    for p, piece in enumerate(pieces):
        feat[p * depth:(p + 1) * depth] = piece[...]
    acc[...] = jnp.zeros_like(acc)
    for c in range(chunks):
        @pl.when(c * CHUNK < live)
        def _():
            fetch(c).wait()

            @pl.loop(0, CHUNK // UNROLL)
            def _(k):
                base = c * CHUNK + k * UNROLL
                products = [
                    jnp.dot(
                        tile_buf[base + u],
                        feat[cols[base + u]],
                        preferred_element_type=jnp.float32,
                    )
                    for u in range(UNROLL)
                ]
                for u in range(UNROLL):
                    acc[rows[base + u]] += products[u]

    out[...] = acc[...].astype(out.dtype)


def spmm(count, rows, cols, tiles, pieces):
    smem = pl.BlockSpec(memory_space=pltpu.SMEM)
    vmem = pl.BlockSpec(memory_space=pltpu.VMEM)
    return pl.pallas_call(
        spmm_kernel,
        out_shape=jax.ShapeDtypeStruct((ROW_TILES, TILE, TILE), jnp.bfloat16),
        in_specs=[smem, smem, smem, pl.BlockSpec(memory_space=pl.ANY)] + [vmem] * 4,
        out_specs=vmem,
        scratch_shapes=[
            pltpu.VMEM((SLOTS, TILE, TILE), jnp.bfloat16),
            pltpu.VMEM((96, TILE, TILE), jnp.bfloat16),
            pltpu.VMEM((ROW_TILES, TILE, TILE), jnp.float32),
            pltpu.SemaphoreType.DMA((SLOTS // CHUNK,)),
        ],
        name="spmm",
    )(count, rows, cols, tiles, *pieces)


def dense_kernel(parts, w_first, b_first, w_second, out):
    total = jnp.sum(parts[...].astype(jnp.float32), axis=0).astype(jnp.bfloat16)
    hidden = jnp.dot(total, w_first[...], preferred_element_type=jnp.float32)
    hidden = jnp.maximum(hidden + b_first[...], 0.0).astype(jnp.bfloat16)
    projected = jnp.dot(hidden, w_second[...], preferred_element_type=jnp.float32)
    out[...] = jnp.broadcast_to(projected.astype(out.dtype)[None], out.shape)


def dense(parts, w_first, b_first, w_second):
    return pl.pallas_call(
        dense_kernel,
        out_shape=jax.ShapeDtypeStruct((4, TILE, TILE), jnp.bfloat16),
        in_specs=[pl.BlockSpec(memory_space=pltpu.VMEM)] * 4,
        out_specs=pl.BlockSpec(memory_space=pltpu.VMEM),
        name="dense",
    )(parts, w_first, b_first[None], w_second)


def gather(copies):
    column = lax.all_to_all(copies, "yh", 0, 0)
    swap = [(0, 1), (1, 0)]
    own = []
    other = []
    for h in range(2):
        half = lax.all_gather(column[2 * h:2 * h + 2], "z", axis=0, tiled=True)
        own.append(half)
        other.append(lax.ppermute(half, "core", swap))
    return own + other


def position(cols):
    core = lax.axis_index("core")
    z = cols // 8
    yh = (cols // 2) % 4
    piece = jnp.where(cols % 2 == core, 0, 2) + yh // 2
    return piece * 24 + z * 2 + yh % 2


def local(features, tiles, tile_index, tile_count, w_first, b_first, w_second, b_second):
    blocks = tiles[0, 0]
    index = tile_index[0, 0]
    count = tile_count[0]
    rows = index // 96
    cols = position(index % 96)

    def aggregate(copies):
        partial = spmm(count, rows, cols, blocks, gather(copies))
        return lax.all_to_all(partial, COL, 0, 0)

    first = aggregate(jnp.broadcast_to(features[None], (4, TILE, TILE)))
    second = aggregate(dense(first, w_first, b_first, w_second))
    return jnp.sum(second.astype(jnp.float32), axis=0) + b_second


def solution(mesh):
    fine = Mesh(mesh.devices.reshape(SIZES), AXES)
    in_specs = (
        P(ROW + COL, None),
        P(ROW, COL, None, None, None),
        P(ROW, COL, None),
        P(ROW, COL),
        P(),
        P(),
        P(),
        P(),
    )
    return jax.shard_map(
        local, mesh=fine, in_specs=in_specs, out_specs=P(ROW + COL, None), check_vma=False
    )
```

```python
import jax
import jax.numpy as jnp
from jax import lax
from jax.experimental import pallas as pl
from jax.experimental.pallas import tpu as pltpu
from jax.sharding import Mesh, PartitionSpec as P

TILE = 128
HALF = 64
ROW_TILES = 8
SLOTS = 128
CHUNK = 16
UNROLL = 8
AXES = ("z", "yh", "core", "x", "yl")
SIZES = (12, 4, 2, 4, 2)
ROW = ("z", "yh", "core")
COL = ("x", "yl")


def spmm_kernel(count, rows, cols, tiles, *rest):
    pieces = rest[:4]
    out, tile_buf, feat, acc, sems = rest[4:]
    live = count[0]
    chunks = SLOTS // CHUNK

    def fetch(c):
        part = pl.ds(c * CHUNK, CHUNK)
        return pltpu.make_async_copy(tiles.at[part], tile_buf.at[part], sems.at[c])

    for c in range(chunks):
        @pl.when(c * CHUNK < live)
        def _():
            fetch(c).start()

    for side in range(2):
        upper, lower = pieces[side], pieces[2 + side]
        feat[48 * side:48 * side + 48, :HALF] = upper[...]

        @pl.loop(0, 12)
        def _(z):
            for yh in range(4):
                feat[48 * side + z * 4 + yh, HALF:] = lower[yh * 12 + z]

    acc[...] = jnp.zeros_like(acc)
    for c in range(chunks):
        @pl.when(c * CHUNK < live)
        def _():
            fetch(c).wait()

            @pl.loop(0, CHUNK // UNROLL)
            def _(k):
                base = c * CHUNK + k * UNROLL
                products = [
                    jnp.dot(
                        tile_buf[base + u],
                        feat[cols[base + u]],
                        preferred_element_type=jnp.float32,
                    )
                    for u in range(UNROLL)
                ]
                for u in range(UNROLL):
                    acc[rows[base + u]] += products[u]

    out[...] = acc[...].astype(out.dtype)


def spmm(count, rows, cols, tiles, pieces):
    smem = pl.BlockSpec(memory_space=pltpu.SMEM)
    vmem = pl.BlockSpec(memory_space=pltpu.VMEM)
    return pl.pallas_call(
        spmm_kernel,
        out_shape=jax.ShapeDtypeStruct((ROW_TILES, TILE, TILE), jnp.bfloat16),
        in_specs=[smem, smem, smem, pl.BlockSpec(memory_space=pl.ANY)] + [vmem] * 4,
        out_specs=vmem,
        scratch_shapes=[
            pltpu.VMEM((SLOTS, TILE, TILE), jnp.bfloat16),
            pltpu.VMEM((96, TILE, TILE), jnp.bfloat16),
            pltpu.VMEM((ROW_TILES, TILE, TILE), jnp.float32),
            pltpu.SemaphoreType.DMA((SLOTS // CHUNK,)),
        ],
        name="spmm",
    )(count, rows, cols, tiles, *pieces)


def dense_kernel(parts, w_first, b_first, w_second, first, second):
    total = jnp.sum(parts[...].astype(jnp.float32), axis=0).astype(jnp.bfloat16)
    hidden = jnp.dot(total, w_first[...], preferred_element_type=jnp.float32)
    hidden = jnp.maximum(hidden + b_first[...], 0.0).astype(jnp.bfloat16)
    projected = jnp.dot(hidden, w_second[...], preferred_element_type=jnp.float32)
    projected = projected.astype(jnp.bfloat16)
    first[...] = projected[:HALF]
    second[...] = jnp.broadcast_to(projected[None, HALF:], second.shape)


def dense(parts, w_first, b_first, w_second):
    return pl.pallas_call(
        dense_kernel,
        out_shape=[
            jax.ShapeDtypeStruct((HALF, TILE), jnp.bfloat16),
            jax.ShapeDtypeStruct((12, HALF, TILE), jnp.bfloat16),
        ],
        in_specs=[pl.BlockSpec(memory_space=pltpu.VMEM)] * 4,
        out_specs=[pl.BlockSpec(memory_space=pltpu.VMEM)] * 2,
        name="dense",
    )(parts, w_first, b_first[None], w_second)


def gather(first, second):
    swap = [(0, 1), (1, 0)]
    lines = lax.all_to_all(second, "z", 0, 0)
    column = lax.all_gather(first, "yh", axis=0)
    spread = lax.all_to_all(jnp.broadcast_to(lines[None], (4,) + lines.shape), "yh", 0, 0)
    upper = lax.all_gather(column, "z", axis=0, tiled=True)
    lower = spread.reshape(48, HALF, TILE)
    return [upper, lax.ppermute(upper, "core", swap), lower, lax.ppermute(lower, "core", swap)]


def position(cols):
    core = lax.axis_index("core")
    return jnp.where(cols % 2 == core, 0, 48) + cols // 2


def local(features, tiles, tile_index, tile_count, w_first, b_first, w_second, b_second):
    blocks = tiles[0, 0]
    index = tile_index[0, 0]
    count = tile_count[0]
    rows = index // 96
    cols = position(index % 96)

    def aggregate(first, second):
        partial = spmm(count, rows, cols, blocks, gather(first, second))
        return lax.all_to_all(partial, COL, 0, 0)

    first = aggregate(features[:HALF], jnp.broadcast_to(features[None, HALF:], (12, HALF, TILE)))
    second = aggregate(*dense(first, w_first, b_first, w_second))
    return jnp.sum(second.astype(jnp.float32), axis=0) + b_second


def solution(mesh):
    fine = Mesh(mesh.devices.reshape(SIZES), AXES)
    in_specs = (
        P(ROW + COL, None),
        P(ROW, COL, None, None, None),
        P(ROW, COL, None),
        P(ROW, COL),
        P(),
        P(),
        P(),
        P(),
    )
    return jax.shard_map(
        local, mesh=fine, in_specs=in_specs, out_specs=P(ROW + COL, None), check_vma=False
    )
```

```python
import jax
import jax.numpy as jnp
from jax import lax
from jax.experimental import pallas as pl
from jax.experimental.pallas import tpu as pltpu
from jax.sharding import Mesh, PartitionSpec as P

TILE = 128
ROW_TILES = 8
SLOTS = 128
CHUNK = 16
UNROLL = 8
AXES = ("zq", "zt", "yh", "core", "x", "yl")
SIZES = (4, 3, 4, 2, 4, 2)
ROW = ("zq", "zt", "yh", "core")
COL = ("x", "yl")


def spmm_kernel(count, rows, cols, tiles, *rest):
    pieces = rest[:6]
    out, tile_buf, feat, acc, sems = rest[6:]
    live = count[0]
    chunks = SLOTS // CHUNK

    def fetch(c):
        part = pl.ds(c * CHUNK, CHUNK)
        return pltpu.make_async_copy(tiles.at[part], tile_buf.at[part], sems.at[c])

    for c in range(chunks):
        @pl.when(c * CHUNK < live)
        def _():
            fetch(c).start()

    for p, piece in enumerate(pieces):
        feat[16 * p:16 * p + 16] = piece[...]
    acc[...] = jnp.zeros_like(acc)
    for c in range(chunks):
        @pl.when(c * CHUNK < live)
        def _():
            fetch(c).wait()

            @pl.loop(0, CHUNK // UNROLL)
            def _(k):
                base = c * CHUNK + k * UNROLL
                products = [
                    jnp.dot(
                        tile_buf[base + u],
                        feat[cols[base + u]],
                        preferred_element_type=jnp.float32,
                    )
                    for u in range(UNROLL)
                ]
                for u in range(UNROLL):
                    acc[rows[base + u]] += products[u]

    out[...] = acc[...].astype(out.dtype)


def spmm(count, rows, cols, tiles, pieces):
    smem = pl.BlockSpec(memory_space=pltpu.SMEM)
    vmem = pl.BlockSpec(memory_space=pltpu.VMEM)
    return pl.pallas_call(
        spmm_kernel,
        out_shape=jax.ShapeDtypeStruct((ROW_TILES, TILE, TILE), jnp.bfloat16),
        in_specs=[smem, smem, smem, pl.BlockSpec(memory_space=pl.ANY)] + [vmem] * 6,
        out_specs=vmem,
        scratch_shapes=[
            pltpu.VMEM((SLOTS, TILE, TILE), jnp.bfloat16),
            pltpu.VMEM((96, TILE, TILE), jnp.bfloat16),
            pltpu.VMEM((ROW_TILES, TILE, TILE), jnp.float32),
            pltpu.SemaphoreType.DMA((SLOTS // CHUNK,)),
        ],
        name="spmm",
    )(count, rows, cols, tiles, *pieces)


def dense_kernel(parts, w_first, b_first, w_second, out):
    total = jnp.sum(parts[...].astype(jnp.float32), axis=0).astype(jnp.bfloat16)
    hidden = jnp.dot(total, w_first[...], preferred_element_type=jnp.float32)
    hidden = jnp.maximum(hidden + b_first[...], 0.0).astype(jnp.bfloat16)
    projected = jnp.dot(hidden, w_second[...], preferred_element_type=jnp.float32)
    out[...] = jnp.broadcast_to(projected.astype(out.dtype)[None], out.shape)


def dense(parts, w_first, b_first, w_second):
    return pl.pallas_call(
        dense_kernel,
        out_shape=jax.ShapeDtypeStruct((16, TILE, TILE), jnp.bfloat16),
        in_specs=[pl.BlockSpec(memory_space=pltpu.VMEM)] * 4,
        out_specs=pl.BlockSpec(memory_space=pltpu.VMEM),
        name="dense",
    )(parts, w_first, b_first[None], w_second)


def gather(copies):
    own = lax.all_to_all(copies, ("zq", "yh"), 0, 0)
    swap = [(0, 1), (1, 0)]
    left = lax.ppermute(own, ("zq", "zt"), [(k, (k + 1) % 12) for k in range(12)])
    right = lax.ppermute(own, ("zq", "zt"), [((k + 1) % 12, k) for k in range(12)])
    pieces = []
    for piece in (own, right, left):
        pieces += [piece, lax.ppermute(piece, "core", swap)]
    return pieces


def position(cols):
    core = lax.axis_index("core")
    third = lax.axis_index("zt")
    z = cols // 8
    side = (z % 3 + 3 - third) % 3
    other = jnp.where(cols % 2 == core, 0, 1)
    return (side * 2 + other) * 16 + z // 3 * 4 + cols // 2 % 4


def local(features, tiles, tile_index, tile_count, w_first, b_first, w_second, b_second):
    blocks = tiles[0, 0]
    index = tile_index[0, 0]
    count = tile_count[0]
    rows = index // 96
    cols = position(index % 96)

    def aggregate(copies):
        partial = spmm(count, rows, cols, blocks, gather(copies))
        return lax.all_to_all(partial, COL, 0, 0)

    first = aggregate(jnp.broadcast_to(features[None], (16, TILE, TILE)))
    second = aggregate(dense(first, w_first, b_first, w_second))
    return jnp.sum(second.astype(jnp.float32), axis=0) + b_second


def solution(mesh):
    fine = Mesh(mesh.devices.reshape(SIZES), AXES)
    in_specs = (
        P(ROW + COL, None),
        P(ROW, COL, None, None, None),
        P(ROW, COL, None),
        P(ROW, COL),
        P(),
        P(),
        P(),
        P(),
    )
    return jax.shard_map(
        local, mesh=fine, in_specs=in_specs, out_specs=P(ROW + COL, None), check_vma=False
    )
```

```python
import jax
import jax.numpy as jnp
from jax import lax
from jax.experimental import pallas as pl
from jax.experimental.pallas import tpu as pltpu
from jax.sharding import Mesh, PartitionSpec as P

TILE = 128
ROW_TILES = 8
SLOTS = 128
CHUNK = 16
UNROLL = 8
AXES = ("zk", "zm", "yh", "core", "x", "yl")
SIZES = (3, 4, 4, 2, 4, 2)
ROW = ("zk", "zm", "yh", "core")
COL = ("x", "yl")


def spmm_kernel(count, rows, cols, tiles, *rest):
    pieces = rest[:10]
    out, tile_buf, feat, acc, sems = rest[10:]
    live = count[0]
    chunks = SLOTS // CHUNK

    def fetch(c):
        part = pl.ds(c * CHUNK, CHUNK)
        return pltpu.make_async_copy(tiles.at[part], tile_buf.at[part], sems.at[c])

    for c in range(chunks):
        @pl.when(c * CHUNK < live)
        def _():
            fetch(c).start()

    at = 0
    for piece in pieces:
        feat[at:at + piece.shape[0]] = piece[...]
        at += piece.shape[0]
    acc[...] = jnp.zeros_like(acc)
    for c in range(chunks):
        @pl.when(c * CHUNK < live)
        def _():
            fetch(c).wait()

            @pl.loop(0, CHUNK // UNROLL)
            def _(k):
                base = c * CHUNK + k * UNROLL
                products = [
                    jnp.dot(
                        tile_buf[base + u],
                        feat[cols[base + u]],
                        preferred_element_type=jnp.float32,
                    )
                    for u in range(UNROLL)
                ]
                for u in range(UNROLL):
                    acc[rows[base + u]] += products[u]

    out[...] = acc[...].astype(out.dtype)


def spmm(count, rows, cols, tiles, pieces):
    smem = pl.BlockSpec(memory_space=pltpu.SMEM)
    vmem = pl.BlockSpec(memory_space=pltpu.VMEM)
    return pl.pallas_call(
        spmm_kernel,
        out_shape=jax.ShapeDtypeStruct((ROW_TILES, TILE, TILE), jnp.bfloat16),
        in_specs=[smem, smem, smem, pl.BlockSpec(memory_space=pl.ANY)] + [vmem] * 10,
        out_specs=vmem,
        scratch_shapes=[
            pltpu.VMEM((SLOTS, TILE, TILE), jnp.bfloat16),
            pltpu.VMEM((96, TILE, TILE), jnp.bfloat16),
            pltpu.VMEM((ROW_TILES, TILE, TILE), jnp.float32),
            pltpu.SemaphoreType.DMA((SLOTS // CHUNK,)),
        ],
        name="spmm",
    )(count, rows, cols, tiles, *pieces)


def dense_kernel(parts, w_first, b_first, w_second, out):
    total = jnp.sum(parts[...].astype(jnp.float32), axis=0).astype(jnp.bfloat16)
    hidden = jnp.dot(total, w_first[...], preferred_element_type=jnp.float32)
    hidden = jnp.maximum(hidden + b_first[...], 0.0).astype(jnp.bfloat16)
    projected = jnp.dot(hidden, w_second[...], preferred_element_type=jnp.float32)
    out[...] = jnp.broadcast_to(projected.astype(out.dtype)[None], out.shape)


def dense(parts, w_first, b_first, w_second):
    return pl.pallas_call(
        dense_kernel,
        out_shape=jax.ShapeDtypeStruct((12, TILE, TILE), jnp.bfloat16),
        in_specs=[pl.BlockSpec(memory_space=pltpu.VMEM)] * 4,
        out_specs=pl.BlockSpec(memory_space=pltpu.VMEM),
        name="dense",
    )(parts, w_first, b_first[None], w_second)


def gather(copies):
    swap = [(0, 1), (1, 0)]
    up = [(k, (k + 1) % 12) for k in range(12)]
    down = [((k + 1) % 12, k) for k in range(12)]
    line = ("zk", "zm")
    own = lax.all_to_all(copies, ("zk", "yh"), 0, 0)
    right = lax.ppermute(own, line, down)
    left = lax.ppermute(own, line, up)
    far = (lax.ppermute(right[:6], line, down), lax.ppermute(left[6:], line, up))
    pieces = [own, right, *far, left]
    return pieces + [lax.ppermute(piece, "core", swap) for piece in pieces]


def position(cols):
    core = lax.axis_index("core")
    side = (cols // 8 + 4 - lax.axis_index("zm")) % 4
    other = jnp.where(cols % 2 == core, 0, 48)
    return other + side * 12 + cols // 32 * 4 + cols // 2 % 4


def local(features, tiles, tile_index, tile_count, w_first, b_first, w_second, b_second):
    blocks = tiles[0, 0]
    index = tile_index[0, 0]
    count = tile_count[0]
    rows = index // 96
    cols = position(index % 96)

    def aggregate(copies):
        partial = spmm(count, rows, cols, blocks, gather(copies))
        return lax.all_to_all(partial, COL, 0, 0)

    first = aggregate(jnp.broadcast_to(features[None], (12, TILE, TILE)))
    second = aggregate(dense(first, w_first, b_first, w_second))
    return jnp.sum(second.astype(jnp.float32), axis=0) + b_second


def solution(mesh):
    fine = Mesh(mesh.devices.reshape(SIZES), AXES)
    in_specs = (
        P(ROW + COL, None),
        P(ROW, COL, None, None, None),
        P(ROW, COL, None),
        P(ROW, COL),
        P(),
        P(),
        P(),
        P(),
    )
    return jax.shard_map(
        local, mesh=fine, in_specs=in_specs, out_specs=P(ROW + COL, None), check_vma=False
    )
```

```python
import functools

import jax
import jax.numpy as jnp
from jax import lax
from jax.experimental import pallas as pl
from jax.experimental.pallas import tpu as pltpu
from jax.sharding import Mesh, PartitionSpec as P

TILE = 128
ROW_TILES = 8
SLOTS = 128
BATCH = 8
GROUP = 32
AXES = ("zq", "zt", "yh", "core", "x", "yl")
SIZES = (4, 3, 4, 2, 4, 2)
ROW = ("zq", "zt", "yh", "core")
COL = ("x", "yl")


def lists_kernel(count, rows, cols, slot_list, row_list, col_list, batches):
    def add(m, sizes):
        col = cols[m]
        group = col // GROUP
        at = jnp.where(group == 0, sizes[0], jnp.where(group == 1, sizes[1], sizes[2]))
        at = at + group * SLOTS
        slot_list[at] = m
        row_list[at] = rows[m]
        col_list[at] = col - group * GROUP
        return tuple(size + (group == g).astype(jnp.int32) for g, size in enumerate(sizes))

    zero = jnp.int32(0)
    sizes = lax.fori_loop(0, count[0], add, (zero, zero, zero))
    for g, size in enumerate(sizes):
        full = (size + BATCH - 1) // BATCH
        batches[g] = full

        @pl.loop(size, full * BATCH)
        def _(at):
            slot_list[g * SLOTS + at] = 0
            row_list[g * SLOTS + at] = ROW_TILES
            col_list[g * SLOTS + at] = 0


def make_lists(count, rows, cols):
    smem = pl.BlockSpec(memory_space=pltpu.SMEM)
    lists = jax.ShapeDtypeStruct((3 * SLOTS,), jnp.int32)
    return pl.pallas_call(
        lists_kernel,
        out_shape=[lists, lists, lists, jax.ShapeDtypeStruct((3,), jnp.int32)],
        in_specs=[smem] * 3,
        out_specs=[smem] * 4,
        name="lists",
    )(count, rows, cols)


def part_kernel(group, slot_list, row_list, col_list, batches, tiles, first, second, *rest):
    if group == 0:
        before, rest = None, rest
    else:
        before, rest = rest[0], rest[1:]
    out, tile_buf, feat, acc, tile_sems, feat_sems = rest
    count = batches[group]
    base = group * SLOTS
    half = GROUP // 2
    moves = [
        pltpu.make_async_copy(first, feat.at[pl.ds(0, half)], feat_sems.at[0]),
        pltpu.make_async_copy(second, feat.at[pl.ds(half, half)], feat_sems.at[1]),
    ]
    for move in moves:
        move.start()

    @pl.loop(0, count)
    def _(b):
        for u in range(BATCH):
            at = b * BATCH + u
            pltpu.make_async_copy(
                tiles.at[slot_list[base + at]], tile_buf.at[at], tile_sems.at[b]
            ).start()

    if before is None:
        acc[:ROW_TILES] = jnp.zeros((ROW_TILES, TILE, TILE), jnp.float32)
    else:
        acc[:ROW_TILES] = before[...]
    for move in moves:
        move.wait()

    @pl.loop(0, count)
    def _(b):
        pltpu.make_async_copy(
            tiles.at[pl.ds(0, BATCH)], tile_buf.at[pl.ds(b * BATCH, BATCH)], tile_sems.at[b]
        ).wait()
        products = [
            jnp.dot(
                tile_buf[b * BATCH + u],
                feat[col_list[base + b * BATCH + u]],
                preferred_element_type=jnp.float32,
            )
            for u in range(BATCH)
        ]
        for u in range(BATCH):
            acc[row_list[base + b * BATCH + u]] += products[u]

    out[...] = acc[:ROW_TILES].astype(out.dtype)


def part(group, lists, tiles, first, second, before=None):
    smem = pl.BlockSpec(memory_space=pltpu.SMEM)
    vmem = pl.BlockSpec(memory_space=pltpu.VMEM)
    away = pl.BlockSpec(memory_space=pl.ANY)
    extra = [] if before is None else [before]
    return pl.pallas_call(
        functools.partial(part_kernel, group),
        out_shape=jax.ShapeDtypeStruct(
            (ROW_TILES, TILE, TILE), jnp.bfloat16 if group == 2 else jnp.float32
        ),
        in_specs=[smem] * 4 + [away] * 3 + [vmem] * len(extra),
        out_specs=vmem,
        scratch_shapes=[
            pltpu.VMEM((SLOTS, TILE, TILE), jnp.bfloat16),
            pltpu.VMEM((GROUP, TILE, TILE), jnp.bfloat16),
            pltpu.VMEM((ROW_TILES + 1, TILE, TILE), jnp.float32),
            pltpu.SemaphoreType.DMA((SLOTS // BATCH,)),
            pltpu.SemaphoreType.DMA((2,)),
        ],
    )(*lists, tiles, first, second, *extra)


def dense_kernel(parts, w_first, b_first, w_second, out):
    total = jnp.sum(parts[...].astype(jnp.float32), axis=0).astype(jnp.bfloat16)
    hidden = jnp.dot(total, w_first[...], preferred_element_type=jnp.float32)
    hidden = jnp.maximum(hidden + b_first[...], 0.0).astype(jnp.bfloat16)
    projected = jnp.dot(hidden, w_second[...], preferred_element_type=jnp.float32)
    out[...] = jnp.broadcast_to(projected.astype(out.dtype)[None], out.shape)


def dense(parts, w_first, b_first, w_second):
    return pl.pallas_call(
        dense_kernel,
        out_shape=jax.ShapeDtypeStruct((16, TILE, TILE), jnp.bfloat16),
        in_specs=[pl.BlockSpec(memory_space=pltpu.VMEM)] * 4,
        out_specs=pl.BlockSpec(memory_space=pltpu.VMEM),
        name="dense",
    )(parts, w_first, b_first[None], w_second)


def position(cols):
    core = lax.axis_index("core")
    third = lax.axis_index("zt")
    z = cols // 8
    side = (z % 3 + 3 - third) % 3
    other = jnp.where(cols % 2 == core, 0, 1)
    piece = jnp.where(side == 0, other, 2 * other + side + 1)
    return piece * 16 + z // 3 * 4 + cols // 2 % 4


def local(features, tiles, tile_index, tile_count, w_first, b_first, w_second, b_second):
    blocks = tiles[0, 0]
    index = tile_index[0, 0]
    count = tile_count[0]
    swap = [(0, 1), (1, 0)]
    up = [(k, (k + 1) % 12) for k in range(12)]
    down = [((k + 1) % 12, k) for k in range(12)]
    lists = None

    def aggregate(copies, lists):
        own = lax.all_to_all(copies, ("zq", "yh"), 0, 0)
        left = lax.ppermute(own, ("zq", "zt"), up)
        right = lax.ppermute(own, ("zq", "zt"), down)
        mid = lax.ppermute(own, "core", swap)
        if lists is None:
            rows = index // 96
            cols = position(index % 96)
            lists = make_lists(count, rows, cols)
        total = part(0, lists, blocks, own, mid)
        left_swap = lax.ppermute(left, "core", swap)
        right_swap = lax.ppermute(right, "core", swap)
        total = part(1, lists, blocks, right, left, total)
        total = part(2, lists, blocks, right_swap, left_swap, total)
        return lax.all_to_all(total, COL, 0, 0), lists

    first, lists = aggregate(jnp.broadcast_to(features[None], (16, TILE, TILE)), None)
    copies = dense(first, w_first, b_first, w_second)
    second, lists = aggregate(copies, lists)
    return jnp.sum(second.astype(jnp.float32), axis=0) + b_second


def solution(mesh):
    fine = Mesh(mesh.devices.reshape(SIZES), AXES)
    in_specs = (
        P(ROW + COL, None),
        P(ROW, COL, None, None, None),
        P(ROW, COL, None),
        P(ROW, COL),
        P(),
        P(),
        P(),
        P(),
    )
    return jax.shard_map(
        local, mesh=fine, in_specs=in_specs, out_specs=P(ROW + COL, None), check_vma=False
    )
```

```python
import jax
import jax.numpy as jnp
from jax import lax
from jax.experimental import pallas as pl
from jax.experimental.pallas import tpu as pltpu
from jax.sharding import Mesh, PartitionSpec as P

TILE = 128
ROW_TILES = 8
SLOTS = 128
CHUNK = 16
UNROLL = 8
AXES = ("zq", "zt", "yh", "core", "x", "yl")
SIZES = (4, 3, 4, 2, 4, 2)
ROW = ("zq", "zt", "yh", "core")
COL = ("x", "yl")


def spmm_kernel(count, rows, cols, tiles, *rest):
    pieces = rest[:6]
    out, tile_buf, feat, acc, tile_sems, feat_sems = rest[6:]
    live = count[0]
    chunks = SLOTS // CHUNK

    def fetch(c):
        part = pl.ds(c * CHUNK, CHUNK)
        return pltpu.make_async_copy(tiles.at[part], tile_buf.at[part], tile_sems.at[c])

    fetch(0).start()
    moves = [
        pltpu.make_async_copy(piece, feat.at[pl.ds(16 * p, 16)], feat_sems.at[p])
        for p, piece in enumerate(pieces)
    ]
    for move in moves:
        move.start()
    for c in range(1, chunks):
        @pl.when(c * CHUNK < live)
        def _():
            fetch(c).start()

    acc[...] = jnp.zeros_like(acc)
    for move in moves:
        move.wait()
    for c in range(chunks):
        def work():
            fetch(c).wait()

            @pl.loop(0, CHUNK // UNROLL)
            def _(k):
                base = c * CHUNK + k * UNROLL
                products = [
                    jnp.dot(
                        tile_buf[base + u],
                        feat[cols[base + u]],
                        preferred_element_type=jnp.float32,
                    )
                    for u in range(UNROLL)
                ]
                for u in range(UNROLL):
                    acc[rows[base + u]] += products[u]

        if c == 0:
            work()
        else:
            pl.when(c * CHUNK < live)(work)

    out[...] = acc[...].astype(out.dtype)


def spmm(count, rows, cols, tiles, pieces):
    smem = pl.BlockSpec(memory_space=pltpu.SMEM)
    away = pl.BlockSpec(memory_space=pl.ANY)
    return pl.pallas_call(
        spmm_kernel,
        out_shape=jax.ShapeDtypeStruct((ROW_TILES, TILE, TILE), jnp.bfloat16),
        in_specs=[smem] * 3 + [away] * 7,
        out_specs=pl.BlockSpec(memory_space=pltpu.VMEM),
        scratch_shapes=[
            pltpu.VMEM((SLOTS, TILE, TILE), jnp.bfloat16),
            pltpu.VMEM((96, TILE, TILE), jnp.bfloat16),
            pltpu.VMEM((ROW_TILES, TILE, TILE), jnp.float32),
            pltpu.SemaphoreType.DMA((SLOTS // CHUNK,)),
            pltpu.SemaphoreType.DMA((6,)),
        ],
        name="spmm",
    )(count, rows, cols, tiles, *pieces)


def dense_kernel(parts, w_first, b_first, w_second, out):
    total = jnp.sum(parts[...].astype(jnp.float32), axis=0).astype(jnp.bfloat16)
    hidden = jnp.dot(total, w_first[...], preferred_element_type=jnp.float32)
    hidden = jnp.maximum(hidden + b_first[...], 0.0).astype(jnp.bfloat16)
    projected = jnp.dot(hidden, w_second[...], preferred_element_type=jnp.float32)
    out[...] = jnp.broadcast_to(projected.astype(out.dtype)[None], out.shape)


def dense(parts, w_first, b_first, w_second):
    return pl.pallas_call(
        dense_kernel,
        out_shape=jax.ShapeDtypeStruct((4, TILE, TILE), jnp.bfloat16),
        in_specs=[pl.BlockSpec(memory_space=pltpu.VMEM)] * 4,
        out_specs=pl.BlockSpec(memory_space=pltpu.VMEM),
        name="dense",
    )(parts, w_first, b_first[None], w_second)


def gather(copies):
    column = lax.all_to_all(copies, "yh", 0, 0)
    own = lax.all_gather(column, "zq", axis=0).reshape(16, TILE, TILE)
    swap = [(0, 1), (1, 0)]
    left = lax.ppermute(own, ("zq", "zt"), [(k, (k + 1) % 12) for k in range(12)])
    right = lax.ppermute(own, ("zq", "zt"), [((k + 1) % 12, k) for k in range(12)])
    pieces = []
    for piece in (own, right, left):
        pieces += [piece, lax.ppermute(piece, "core", swap)]
    return pieces


def position(cols):
    core = lax.axis_index("core")
    third = lax.axis_index("zt")
    z = cols // 8
    side = (z % 3 + 3 - third) % 3
    other = jnp.where(cols % 2 == core, 0, 1)
    return (side * 2 + other) * 16 + z // 3 * 4 + cols // 2 % 4


def local(features, tiles, tile_index, tile_count, w_first, b_first, w_second, b_second):
    blocks = tiles[0, 0]
    index = tile_index[0, 0]
    count = tile_count[0]
    rows = index // 96
    cols = position(index % 96)

    def aggregate(copies):
        partial = spmm(count, rows, cols, blocks, gather(copies))
        return lax.all_to_all(partial, COL, 0, 0)

    first = aggregate(jnp.broadcast_to(features[None], (4, TILE, TILE)))
    second = aggregate(dense(first, w_first, b_first, w_second))
    return jnp.sum(second.astype(jnp.float32), axis=0) + b_second


def solution(mesh):
    fine = Mesh(mesh.devices.reshape(SIZES), AXES)
    in_specs = (
        P(ROW + COL, None),
        P(ROW, COL, None, None, None),
        P(ROW, COL, None),
        P(ROW, COL),
        P(),
        P(),
        P(),
        P(),
    )
    return jax.shard_map(
        local, mesh=fine, in_specs=in_specs, out_specs=P(ROW + COL, None), check_vma=False
    )
```

```python
import functools

import jax
import jax.numpy as jnp
from jax import lax
from jax.experimental import pallas as pl
from jax.experimental.pallas import tpu as pltpu
from jax.sharding import Mesh, PartitionSpec as P

TILE = 128
ROW_TILES = 8
SLOTS = 128
CHUNKS = ((0, 16), (16, 16), (32, 32), (64, 32), (96, 32))
AXES = ("zq", "zt", "yh", "core", "x", "yl")
SIZES = (4, 3, 4, 2, 4, 2)
ROW = ("zq", "zt", "yh", "core")
COL = ("x", "yl")


def in_vmem(x):
    return pltpu.with_memory_space_constraint(x, pltpu.VMEM)


def spmm_kernel(count, rows, cols, tiles, *rest):
    pieces = rest[:6]
    out, tile_buf, feat, acc, tile_sems = rest[6:]
    live = count[0]

    def fetch(c):
        part = pl.ds(*CHUNKS[c])
        return pltpu.make_async_copy(tiles.at[part], tile_buf.at[part], tile_sems.at[c])

    def work(c):
        fetch(c).wait()
        start, size = CHUNKS[c]
        for u in range(start, start + size):
            acc[rows[u]] += jnp.dot(
                tile_buf[u], feat[cols[u]], preferred_element_type=jnp.float32
            )

    fetch(0).start()
    for c in range(1, len(CHUNKS)):
        pl.when(CHUNKS[c][0] < live)(fetch(c).start)

    acc[...] = jnp.zeros_like(acc)
    for p, piece in enumerate(pieces):
        feat[16 * p:16 * p + 16] = piece[...]
    work(0)
    for c in range(1, len(CHUNKS)):
        pl.when(CHUNKS[c][0] < live)(functools.partial(work, c))
    out[...] = acc[...].astype(out.dtype)


def spmm(count, rows, cols, tiles, pieces):
    smem = pl.BlockSpec(memory_space=pltpu.SMEM)
    vmem = pl.BlockSpec(memory_space=pltpu.VMEM)
    return pl.pallas_call(
        spmm_kernel,
        out_shape=jax.ShapeDtypeStruct((ROW_TILES, TILE, TILE), jnp.bfloat16),
        in_specs=[smem] * 3 + [pl.BlockSpec(memory_space=pl.ANY)] + [vmem] * 6,
        out_specs=vmem,
        scratch_shapes=[
            pltpu.VMEM((SLOTS, TILE, TILE), jnp.bfloat16),
            pltpu.VMEM((96, TILE, TILE), jnp.bfloat16),
            pltpu.VMEM((ROW_TILES, TILE, TILE), jnp.float32),
            pltpu.SemaphoreType.DMA((len(CHUNKS),)),
        ],
        compiler_params=pltpu.CompilerParams(vmem_limit_bytes=12 << 20),
        name="spmm",
    )(
        count,
        rows,
        cols,
        pltpu.with_memory_space_constraint(tiles, pltpu.HBM),
        *(in_vmem(piece) for piece in pieces),
    )


def dense_kernel(parts, w_first, b_first, w_second, out):
    total = jnp.sum(parts[...].astype(jnp.float32), axis=0).astype(jnp.bfloat16)
    hidden = jnp.dot(total, w_first[...], preferred_element_type=jnp.float32)
    hidden = jnp.maximum(hidden + b_first[...], 0.0).astype(jnp.bfloat16)
    projected = jnp.dot(hidden, w_second[...], preferred_element_type=jnp.float32)
    out[...] = jnp.broadcast_to(projected.astype(out.dtype)[None], out.shape)


def dense(parts, w_first, b_first, w_second):
    return pl.pallas_call(
        dense_kernel,
        out_shape=jax.ShapeDtypeStruct((4, TILE, TILE), jnp.bfloat16),
        in_specs=[pl.BlockSpec(memory_space=pltpu.VMEM)] * 4,
        out_specs=pl.BlockSpec(memory_space=pltpu.VMEM),
        compiler_params=pltpu.CompilerParams(vmem_limit_bytes=8 << 20),
        name="dense",
    )(*(in_vmem(x) for x in (parts, w_first, b_first[None], w_second)))


def gather(copies):
    column = lax.all_to_all(copies, "yh", 0, 0)
    own = lax.all_gather(column, "zq", axis=0).reshape(16, TILE, TILE)
    swap = [(0, 1), (1, 0)]
    left = lax.ppermute(own, ("zq", "zt"), [(k, (k + 1) % 12) for k in range(12)])
    right = lax.ppermute(own, ("zq", "zt"), [((k + 1) % 12, k) for k in range(12)])
    pieces = []
    for piece in (own, right, left):
        pieces += [piece, lax.ppermute(piece, "core", swap)]
    return pieces


def position(cols):
    core = lax.axis_index("core")
    third = lax.axis_index("zt")
    z = cols // 8
    side = (z % 3 + 3 - third) % 3
    other = jnp.where(cols % 2 == core, 0, 1)
    return (side * 2 + other) * 16 + z // 3 * 4 + cols // 2 % 4


def local(features, tiles, tile_index, tile_count, w_first, b_first, w_second, b_second):
    blocks = tiles[0, 0]
    index = tile_index[0, 0]
    count = tile_count[0]
    rows = index // 96
    cols = position(index % 96)

    def aggregate(copies):
        partial = spmm(count, rows, cols, blocks, gather(copies))
        return lax.all_to_all(partial, COL, 0, 0)

    first = aggregate(jnp.broadcast_to(features[None], (4, TILE, TILE)))
    second = aggregate(dense(first, w_first, b_first, w_second))
    return jnp.sum(second.astype(jnp.float32), axis=0) + b_second


def solution(mesh):
    fine = Mesh(mesh.devices.reshape(SIZES), AXES)
    in_specs = (
        P(ROW + COL, None),
        P(ROW, COL, None, None, None),
        P(ROW, COL, None),
        P(ROW, COL),
        P(),
        P(),
        P(),
        P(),
    )
    return jax.shard_map(
        local, mesh=fine, in_specs=in_specs, out_specs=P(ROW + COL, None), check_vma=False
    )
```

```python
import functools

import jax
import jax.numpy as jnp
from jax import lax
from jax.experimental import pallas as pl
from jax.experimental.pallas import tpu as pltpu
from jax.sharding import Mesh, PartitionSpec as P

TILE = 128
ROW_TILES = 8
SLOTS = 128
CHUNKS = ((0, 16), (16, 16), (32, 32), (64, 32), (96, 32))
AXES = ("zq", "zt", "yh", "core", "x", "yl")
SIZES = (4, 3, 4, 2, 4, 2)
ROW = ("zq", "zt", "yh", "core")
COL = ("x", "yl")


def in_vmem(x):
    return pltpu.with_memory_space_constraint(x, pltpu.VMEM)


def spmm_kernel(count, rows, cols, tiles, *rest):
    pieces = rest[:6]
    out, tile_buf, feat, acc, tile_sems = rest[6:]
    live = count[0]

    def fetch(c):
        part = pl.ds(*CHUNKS[c])
        return pltpu.make_async_copy(tiles.at[part], tile_buf.at[part], tile_sems.at[c])

    def work(c):
        fetch(c).wait()
        start, size = CHUNKS[c]
        for u in range(start, start + size):
            acc[rows[u]] += jnp.dot(
                tile_buf[u], feat[cols[u]], preferred_element_type=jnp.float32
            )

    fetch(0).start()
    for c in range(1, len(CHUNKS)):
        pl.when(CHUNKS[c][0] < live)(fetch(c).start)

    acc[...] = jnp.zeros_like(acc)
    for p, piece in enumerate(pieces):
        feat[16 * p:16 * p + 16] = piece[...]
    work(0)
    for c in range(1, len(CHUNKS)):
        pl.when(CHUNKS[c][0] < live)(functools.partial(work, c))
    out[...] = acc[...].astype(out.dtype)


def spmm(count, rows, cols, tiles, pieces):
    smem = pl.BlockSpec(memory_space=pltpu.SMEM)
    vmem = pl.BlockSpec(memory_space=pltpu.VMEM)
    return pl.pallas_call(
        spmm_kernel,
        out_shape=jax.ShapeDtypeStruct((ROW_TILES, TILE, TILE), jnp.bfloat16),
        in_specs=[smem] * 3 + [pl.BlockSpec(memory_space=pl.ANY)] + [vmem] * 6,
        out_specs=vmem,
        scratch_shapes=[
            pltpu.VMEM((SLOTS, TILE, TILE), jnp.bfloat16),
            pltpu.VMEM((96, TILE, TILE), jnp.bfloat16),
            pltpu.VMEM((ROW_TILES, TILE, TILE), jnp.float32),
            pltpu.SemaphoreType.DMA((len(CHUNKS),)),
        ],
        compiler_params=pltpu.CompilerParams(vmem_limit_bytes=12 << 20),
        name="spmm",
    )(
        count,
        rows,
        cols,
        pltpu.with_memory_space_constraint(tiles, pltpu.HBM),
        *(in_vmem(piece) for piece in pieces),
    )


def dense_kernel(parts, w_first, b_first, w_second, out):
    total = jnp.sum(parts[...].astype(jnp.float32), axis=0).astype(jnp.bfloat16)
    hidden = jnp.dot(total, w_first[...], preferred_element_type=jnp.float32)
    hidden = jnp.maximum(hidden + b_first[...], 0.0).astype(jnp.bfloat16)
    projected = jnp.dot(hidden, w_second[...], preferred_element_type=jnp.float32)
    out[...] = jnp.broadcast_to(projected.astype(out.dtype)[None], out.shape)


def dense(parts, w_first, b_first, w_second):
    return pl.pallas_call(
        dense_kernel,
        out_shape=jax.ShapeDtypeStruct((4, TILE, TILE), jnp.bfloat16),
        in_specs=[pl.BlockSpec(memory_space=pltpu.VMEM)] * 4,
        out_specs=pl.BlockSpec(memory_space=pltpu.VMEM),
        compiler_params=pltpu.CompilerParams(vmem_limit_bytes=8 << 20),
        name="dense",
    )(*(in_vmem(x) for x in (parts, w_first, b_first[None], w_second)))


def gather(copies):
    column = lax.all_to_all(copies, "yh", 0, 0)
    own = lax.all_gather(column, "zq", axis=0).reshape(16, TILE, TILE)
    swap = [(0, 1), (1, 0)]
    line = ("zq", "zt", "core")
    crossed = []
    for flip in range(2):
        step = [1, -1] if flip == 0 else [-1, 1]
        pairs = [(2 * z + c, (z + step[c]) % 12 * 2 + c) for z in range(12) for c in range(2)]
        crossed.append(lax.ppermute(own, line, pairs))
    pieces = []
    for piece in (own, *crossed):
        pieces += [piece, lax.ppermute(piece, "core", swap)]
    return pieces


def position(cols):
    core = lax.axis_index("core")
    third = lax.axis_index("zt")
    z = cols // 8
    source = cols % 2
    side = (z % 3 + 3 - third) % 3
    first = (side == 2) == (source == 0)
    piece = jnp.where(side == 0, 0, jnp.where(first, 2, 4)) + jnp.where(source == core, 0, 1)
    return piece * 16 + z // 3 * 4 + cols // 2 % 4


def local(features, tiles, tile_index, tile_count, w_first, b_first, w_second, b_second):
    blocks = tiles[0, 0]
    index = tile_index[0, 0]
    count = tile_count[0]
    rows = index // 96
    cols = position(index % 96)

    def aggregate(copies):
        partial = spmm(count, rows, cols, blocks, gather(copies))
        return lax.all_to_all(partial, COL, 0, 0)

    first = aggregate(jnp.broadcast_to(features[None], (4, TILE, TILE)))
    second = aggregate(dense(first, w_first, b_first, w_second))
    return jnp.sum(second.astype(jnp.float32), axis=0) + b_second


def solution(mesh):
    fine = Mesh(mesh.devices.reshape(SIZES), AXES)
    in_specs = (
        P(ROW + COL, None),
        P(ROW, COL, None, None, None),
        P(ROW, COL, None),
        P(ROW, COL),
        P(),
        P(),
        P(),
        P(),
    )
    return jax.shard_map(
        local, mesh=fine, in_specs=in_specs, out_specs=P(ROW + COL, None), check_vma=False
    )
```

```python
import functools

import jax
import jax.numpy as jnp
from jax import lax
from jax.experimental import pallas as pl
from jax.experimental.pallas import tpu as pltpu
from jax.sharding import Mesh, PartitionSpec as P

TILE = 128
ROW_TILES = 8
SLOTS = 128
CHUNKS = ((0, 16), (16, 16), (32, 32), (64, 32), (96, 32))
AXES = ("zq", "zt", "yh", "core", "x", "yl")
SIZES = (4, 3, 4, 2, 4, 2)
ROW = ("zq", "zt", "yh", "core")
COL = ("x", "yl")


def in_vmem(x):
    return pltpu.with_memory_space_constraint(x, pltpu.VMEM)


def spmm_kernel(count, rows, cols, tiles, *rest):
    pieces = rest[:6]
    out, tile_buf, feat, acc, tile_sems = rest[6:]
    live = count[0]

    def fetch(c):
        part = pl.ds(*CHUNKS[c])
        return pltpu.make_async_copy(tiles.at[part], tile_buf.at[part], tile_sems.at[c])

    def work(c):
        fetch(c).wait()
        start, size = CHUNKS[c]
        for u in range(start, start + size):
            acc[rows[u]] += jnp.dot(
                tile_buf[u], feat[cols[u]], preferred_element_type=jnp.float32
            )

    fetch(0).start()
    for c in range(1, len(CHUNKS)):
        pl.when(CHUNKS[c][0] < live)(fetch(c).start)

    acc[...] = jnp.zeros_like(acc)
    for p, piece in enumerate(pieces):
        feat[16 * p:16 * p + 16] = piece[...]
    work(0)
    for c in range(1, len(CHUNKS)):
        pl.when(CHUNKS[c][0] < live)(functools.partial(work, c))
    out[...] = acc[...].astype(out.dtype)


def spmm(count, rows, cols, tiles, pieces):
    smem = pl.BlockSpec(memory_space=pltpu.SMEM)
    vmem = pl.BlockSpec(memory_space=pltpu.VMEM)
    return pl.pallas_call(
        spmm_kernel,
        out_shape=jax.ShapeDtypeStruct((ROW_TILES, TILE, TILE), jnp.bfloat16),
        in_specs=[smem] * 3 + [pl.BlockSpec(memory_space=pl.ANY)] + [vmem] * 6,
        out_specs=vmem,
        scratch_shapes=[
            pltpu.VMEM((SLOTS, TILE, TILE), jnp.bfloat16),
            pltpu.VMEM((96, TILE, TILE), jnp.bfloat16),
            pltpu.VMEM((ROW_TILES, TILE, TILE), jnp.float32),
            pltpu.SemaphoreType.DMA((len(CHUNKS),)),
        ],
        compiler_params=pltpu.CompilerParams(vmem_limit_bytes=12 << 20),
        name="spmm",
    )(
        count,
        rows,
        cols,
        pltpu.with_memory_space_constraint(tiles, pltpu.HBM),
        *(in_vmem(piece) for piece in pieces),
    )


def dense_kernel(parts, w_first, b_first, w_second, out):
    total = jnp.sum(parts[...].astype(jnp.float32), axis=0).astype(jnp.bfloat16)
    hidden = jnp.dot(total, w_first[...], preferred_element_type=jnp.float32)
    hidden = jnp.maximum(hidden + b_first[...], 0.0).astype(jnp.bfloat16)
    projected = jnp.dot(hidden, w_second[...], preferred_element_type=jnp.float32)
    out[...] = projected.astype(out.dtype)


def dense(parts, w_first, b_first, w_second):
    return pl.pallas_call(
        dense_kernel,
        out_shape=jax.ShapeDtypeStruct((TILE, TILE), jnp.bfloat16),
        in_specs=[pl.BlockSpec(memory_space=pltpu.VMEM)] * 4,
        out_specs=pl.BlockSpec(memory_space=pltpu.VMEM),
        compiler_params=pltpu.CompilerParams(vmem_limit_bytes=8 << 20),
        name="dense",
    )(*(in_vmem(x) for x in (parts, w_first, b_first[None], w_second)))


def gather(block):
    column = lax.all_gather(block, "yh", axis=0)
    own = lax.all_gather(column, "zq", axis=0).reshape(16, TILE, TILE)
    swap = [(0, 1), (1, 0)]
    left = lax.ppermute(own, ("zq", "zt"), [(k, (k + 1) % 12) for k in range(12)])
    right = lax.ppermute(own, ("zq", "zt"), [((k + 1) % 12, k) for k in range(12)])
    pieces = []
    for piece in (own, right, left):
        pieces += [piece, lax.ppermute(piece, "core", swap)]
    return pieces


def position(cols):
    core = lax.axis_index("core")
    third = lax.axis_index("zt")
    z = cols // 8
    side = (z % 3 + 3 - third) % 3
    other = jnp.where(cols % 2 == core, 0, 1)
    return (side * 2 + other) * 16 + z // 3 * 4 + cols // 2 % 4


def local(features, tiles, tile_index, tile_count, w_first, b_first, w_second, b_second):
    blocks = tiles[0, 0]
    index = tile_index[0, 0]
    count = tile_count[0]
    rows = index // 96
    cols = position(index % 96)

    def aggregate(block):
        partial = spmm(count, rows, cols, blocks, gather(block))
        return lax.all_to_all(partial, COL, 0, 0)

    first = aggregate(features)
    second = aggregate(dense(first, w_first, b_first, w_second))
    return jnp.sum(second.astype(jnp.float32), axis=0) + b_second


def solution(mesh):
    fine = Mesh(mesh.devices.reshape(SIZES), AXES)
    in_specs = (
        P(ROW + COL, None),
        P(ROW, COL, None, None, None),
        P(ROW, COL, None),
        P(ROW, COL),
        P(),
        P(),
        P(),
        P(),
    )
    return jax.shard_map(
        local, mesh=fine, in_specs=in_specs, out_specs=P(ROW + COL, None), check_vma=False
    )
```

```python
import functools

import jax
import jax.numpy as jnp
from jax import lax
from jax.experimental import pallas as pl
from jax.experimental.pallas import tpu as pltpu
from jax.sharding import Mesh, PartitionSpec as P

TILE = 128
ROW_TILES = 8
SLOTS = 128
CHUNKS = ((0, 16), (16, 16), (32, 32), (64, 32), (96, 32))
AXES = ("zq", "zt", "yh", "core", "x", "yl")
SIZES = (4, 3, 4, 2, 4, 2)
ROW = ("zq", "zt", "yh", "core")
COL = ("x", "yl")


def in_vmem(x):
    return pltpu.with_memory_space_constraint(x, pltpu.VMEM)


def spmm_kernel(count, rows, cols, tiles, *rest):
    pieces = rest[:6]
    out, tile_buf, feat, *accs, tile_sems = rest[6:]
    live = count[0]

    def fetch(c):
        part = pl.ds(*CHUNKS[c])
        return pltpu.make_async_copy(tiles.at[part], tile_buf.at[part], tile_sems.at[c])

    def work(c):
        fetch(c).wait()
        start, size = CHUNKS[c]
        for u in range(start, start + size):
            accs[u % 2][rows[u]] += jnp.dot(
                tile_buf[u], feat[cols[u]], preferred_element_type=jnp.float32
            )

    fetch(0).start()
    for c in range(1, len(CHUNKS)):
        pl.when(CHUNKS[c][0] < live)(fetch(c).start)

    for acc in accs:
        acc[...] = jnp.zeros_like(acc)
    for p, piece in enumerate(pieces):
        feat[16 * p:16 * p + 16] = piece[...]
    work(0)
    for c in range(1, len(CHUNKS)):
        pl.when(CHUNKS[c][0] < live)(functools.partial(work, c))
    out[...] = (accs[0][...] + accs[1][...]).astype(out.dtype)


def spmm(count, rows, cols, tiles, pieces):
    smem = pl.BlockSpec(memory_space=pltpu.SMEM)
    vmem = pl.BlockSpec(memory_space=pltpu.VMEM)
    return pl.pallas_call(
        spmm_kernel,
        out_shape=jax.ShapeDtypeStruct((ROW_TILES, TILE, TILE), jnp.bfloat16),
        in_specs=[smem] * 3 + [pl.BlockSpec(memory_space=pl.ANY)] + [vmem] * 6,
        out_specs=vmem,
        scratch_shapes=[
            pltpu.VMEM((SLOTS, TILE, TILE), jnp.bfloat16),
            pltpu.VMEM((96, TILE, TILE), jnp.bfloat16),
            pltpu.VMEM((ROW_TILES, TILE, TILE), jnp.float32),
            pltpu.VMEM((ROW_TILES, TILE, TILE), jnp.float32),
            pltpu.SemaphoreType.DMA((len(CHUNKS),)),
        ],
        compiler_params=pltpu.CompilerParams(vmem_limit_bytes=12 << 20),
        name="spmm",
    )(
        count,
        rows,
        cols,
        pltpu.with_memory_space_constraint(tiles, pltpu.HBM),
        *(in_vmem(piece) for piece in pieces),
    )


def dense_kernel(parts, w_first, b_first, w_second, out):
    total = jnp.sum(parts[...].astype(jnp.float32), axis=0).astype(jnp.bfloat16)
    hidden = jnp.dot(total, w_first[...], preferred_element_type=jnp.float32)
    hidden = jnp.maximum(hidden + b_first[...], 0.0).astype(jnp.bfloat16)
    projected = jnp.dot(hidden, w_second[...], preferred_element_type=jnp.float32)
    out[...] = projected.astype(out.dtype)


def dense(parts, w_first, b_first, w_second):
    return pl.pallas_call(
        dense_kernel,
        out_shape=jax.ShapeDtypeStruct((TILE, TILE), jnp.bfloat16),
        in_specs=[pl.BlockSpec(memory_space=pltpu.VMEM)] * 4,
        out_specs=pl.BlockSpec(memory_space=pltpu.VMEM),
        compiler_params=pltpu.CompilerParams(vmem_limit_bytes=8 << 20),
        name="dense",
    )(*(in_vmem(x) for x in (parts, w_first, b_first[None], w_second)))


def gather(block):
    column = lax.all_gather(block, "yh", axis=0, tiled=True)
    own = lax.all_gather(column, "zq", axis=0, tiled=True).reshape(16, TILE, TILE)
    swap = [(0, 1), (1, 0)]
    left = lax.ppermute(own, ("zq", "zt"), [(k, (k + 1) % 12) for k in range(12)])
    right = lax.ppermute(own, ("zq", "zt"), [((k + 1) % 12, k) for k in range(12)])
    pieces = []
    for piece in (own, right, left):
        pieces += [piece, lax.ppermute(piece, "core", swap)]
    return pieces


def position(cols):
    core = lax.axis_index("core")
    third = lax.axis_index("zt")
    z = cols // 8
    side = (z % 3 + 3 - third) % 3
    other = jnp.where(cols % 2 == core, 0, 1)
    return (side * 2 + other) * 16 + z // 3 * 4 + cols // 2 % 4


def local(features, tiles, tile_index, tile_count, w_first, b_first, w_second, b_second):
    blocks = tiles[0, 0]
    index = tile_index[0, 0]
    count = tile_count[0]
    rows = index // 96
    cols = position(index % 96)

    def aggregate(block):
        partial = spmm(count, rows, cols, blocks, gather(block))
        return lax.all_to_all(partial, COL, 0, 0)

    first = aggregate(features)
    second = aggregate(dense(first, w_first, b_first, w_second))
    return jnp.sum(second.astype(jnp.float32), axis=0) + b_second


def solution(mesh):
    fine = Mesh(mesh.devices.reshape(SIZES), AXES)
    in_specs = (
        P(ROW + COL, None),
        P(ROW, COL, None, None, None),
        P(ROW, COL, None),
        P(ROW, COL),
        P(),
        P(),
        P(),
        P(),
    )
    return jax.shard_map(
        local, mesh=fine, in_specs=in_specs, out_specs=P(ROW + COL, None), check_vma=False
    )
```
